512 devices in a mesh: gz: 16 (over z, core), xy: 32 (over y, x).
Axes of the slice: x: 4, y: 8, z: 8, core: 2. Of those that a mesh axis runs over, the one named last changes fastest.
Arguments:
- positions: float32 [3, 65536], P(None, ('gz', 'xy')), may hold values from 0 to 64, as said below
- velocities: float32 [3, 65536], P(None, ('gz', 'xy')), may hold values from -6 to 6
- forces: float32 [3, 65536], P(None, ('gz', 'xy')), may hold values from -6 to 6
- species: int32 [65536], P(('gz', 'xy')), may hold values from 0 to 3
- counts: int32 [512], P(('gz', 'xy')), may hold values from 16 to 128, as said below
- neighbours: int32 [24, 65536], P(None, ('gz', 'xy')), may hold values from 0 to 320, as said below
- send_inplane: int32 [2, 16384], P(None, ('gz', 'xy')), may hold values from 0 to 127
- send_normal: int32 [2, 32768], P(None, ('gz', 'xy')), may hold values from 0 to 191
- embedding: float32 [4, 128], replicated, may hold values from -6 to 6
- inverse_mass: float32 [4], replicated, may hold values from 0.25 to 1
- radial_weight: float32 [16, 128], replicated, may hold values from -1.5 to 1.5
- mix_weight: float32 [128, 128], replicated, may hold values from -0.5 to 0.5
- self_weight: float32 [128, 128], replicated, may hold values from -0.5 to 0.5
- charge_weight: float32 [128, 128], replicated, may hold values from -0.5 to 0.5
- readout_weight: float32 [128, 128], replicated, may hold values from -0.5 to 0.5
- readout_vector: float32 [128], replicated, may hold values from -0.5 to 0.5
- kernel_filter: float32 [512, 128], replicated, may hold values from 0.2 to 2
Outputs:
- positions_new: float32 [3, 65536], P(None, ('gz', 'xy'))
- velocities_new: float32 [3, 65536], P(None, ('gz', 'xy'))
- forces_new: float32 [3, 65536], P(None, ('gz', 'xy'))
- energy: float32 [], replicated
The draws below stay inside these ranges and needn't reach their ends.
Inputs may be any that keep to these rules, and one draw needn't show every extreme that they name: `positions`: coordinates of domain (g, p) lie in [2 p, 2 p + 2) x [0, 4) x [2 g, 2 g + 2). `counts`: the first domain is full; filling falls along the slab-normal axis. `neighbours`: slots of the extended list: own 128, then 32 from the lower and 32 from the upper in-plane neighbour, 64 from the lower and 64 from the upper slab-normal neighbour, then the padding slot 320.
All inputs are finite; a program needn't handle non-finite values.
Results may differ from the reference program's by a relative error of at most 0.0003.
Values sent between devices are 32-bit elements; how exact they have to be, the bound alone decides.
A program may use at most 64 MiB of HBM per device.

```python
import math
import jax
import jax.numpy as jnp
from jax import lax

C = 128
KGRID = 8
NB = 16
SPECIES = 4
NEIGH = 24
ATOMS_DEV = 128
NK = 512
GXY = 32
GGZ = 64
EXT = 321
DOMAINS = 512
ATOMS = 65536
N_GZ = 16
N_XY = 32


def draw_positions(key, part):
    all_atoms = ATOMS_DEV * N_GZ * N_XY
    column = jnp.arange(all_atoms)
    domain = column // ATOMS_DEV
    layer_index = (domain // N_XY).astype(jnp.float32)
    strip_index = (domain % N_XY).astype(jnp.float32)
    uniform_draw = jax.random.uniform(key, (3, all_atoms), jnp.float32)
    along_x = (strip_index + uniform_draw[0]) * 2.0
    along_y = uniform_draw[1] * 4.0
    along_z = (layer_index + uniform_draw[2]) * 2.0
    return jnp.stack([along_x, along_y, along_z], axis=0).astype(jnp.float32)


def draw_counts(key, part):
    domain = jnp.arange(N_GZ * N_XY)
    layer_index = domain // N_XY
    dropped = jax.random.randint(key, (N_GZ * N_XY,), 0, ATOMS_DEV // 4 + 1)
    baseline = ATOMS_DEV - layer_index * ATOMS_DEV * 3 // (4 * N_GZ)
    filled = jnp.maximum(baseline - dropped, ATOMS_DEV // 8)
    return jnp.where(domain == 0, ATOMS_DEV, filled).astype(jnp.int32)


def draw_neighbours(key, part):
    all_atoms = ATOMS_DEV * N_GZ * N_XY
    key_first = jax.random.fold_in(key, 11)
    key_second = jax.random.fold_in(key, 23)
    chosen = jax.random.randint(key_first, (NEIGH, all_atoms), 0, EXT - 1)
    filled = jax.random.randint(key_second, (all_atoms,), NEIGH // 2, NEIGH + 1)
    slot_index = jnp.arange(NEIGH)[:, None]
    return jnp.where(slot_index < filled[None, :], chosen, EXT - 1).astype(jnp.int32)


def place_ends(drawn, rng, least, top_value):
    longest = drawn.shape.index(max(drawn.shape))
    spots = []
    for shift in (0, 1):
        where = [jax.random.randint(jax.random.fold_in(rng, axis), (), 0, length) for axis, length in enumerate(drawn.shape)]
        where[longest] = (where[longest] + shift) % drawn.shape[longest]
        spots.append(tuple(where))
    return drawn.at[spots[0]].set(least).at[spots[1]].set(top_value)


def level_of(rng, dims, cuts, least, top_value):
    factor_of, own = 1.0, jax.random.fold_in(rng, 6)
    for position, parts in cuts:
        steps = jnp.exp(jax.random.uniform(jax.random.fold_in(own, position), (parts,), jnp.float32, least / len(cuts), top_value / len(cuts)))
        factor_of = factor_of * jnp.repeat(steps, dims[position] // parts).reshape([-1 if axis == position else 1 for axis in range(len(dims))])
    return factor_of


def noise(own_key, dims, width, bound, cuts=(), kind=jnp.bfloat16):
    values = width * jax.random.normal(own_key, dims, jnp.float32)
    if cuts:
        values = values * level_of(own_key, dims, cuts, -0.22, 0.18)
    return jnp.clip(values, -bound, bound).astype(kind)


def setup_inputs(seed: int = 0) -> dict:
    key_of = jax.random.split(jax.random.key(seed), 18)
    positions = draw_positions(jax.random.fold_in(key_of[17], 71), 0)
    velocities = noise(key_of[1], (3, ATOMS), 1.0, 6.0, ((1, 512),), jnp.float32)
    forces = noise(key_of[2], (3, ATOMS), 1.0, 6.0, ((1, 512),), jnp.float32)
    species = place_ends(jax.random.randint(key_of[3], (ATOMS,), 0, SPECIES), jax.random.fold_in(key_of[3], 1), 0, SPECIES - 1).astype(jnp.int32)
    counts = draw_counts(jax.random.fold_in(key_of[17], 71), 0)
    neighbours = draw_neighbours(jax.random.fold_in(key_of[17], 71), 0)
    send_inplane = place_ends(jax.random.randint(key_of[6], (2, DOMAINS * GXY), 0, ATOMS_DEV), jax.random.fold_in(key_of[6], 1), 0, ATOMS_DEV - 1).astype(jnp.int32)
    send_normal = place_ends(jax.random.randint(key_of[7], (2, DOMAINS * GGZ), 0, ATOMS_DEV + 2 * GXY), jax.random.fold_in(key_of[7], 1), 0, (ATOMS_DEV + 2 * GXY) - 1).astype(jnp.int32)
    embedding = noise(key_of[8], (SPECIES, C), 1.0, 6.0, (), jnp.float32)
    inverse_mass = jnp.clip(jnp.exp(jax.random.uniform(key_of[9], (SPECIES,), jnp.float32, math.log(0.25), math.log(1.0))), 0.25, 1.0)
    radial_weight = noise(key_of[10], (NB, C), NB ** -0.5, 1.5, (), jnp.float32)
    mix_weight = noise(key_of[11], (C, C), C ** -0.5, 0.5, (), jnp.float32)
    self_weight = noise(key_of[12], (C, C), C ** -0.5, 0.5, (), jnp.float32)
    charge_weight = noise(key_of[13], (C, C), C ** -0.5, 0.5, (), jnp.float32)
    readout_weight = noise(key_of[14], (C, C), C ** -0.5, 0.5, (), jnp.float32)
    readout_vector = noise(key_of[15], (C,), C ** -0.5, 0.5, (), jnp.float32)
    kernel_filter = jnp.clip(jnp.exp(jax.random.uniform(key_of[16], (NK, C), jnp.float32, math.log(0.2), math.log(2.0))), 0.2, 2.0)
    return {"positions": positions, "velocities": velocities, "forces": forces, "species": species, "counts": counts, "neighbours": neighbours, "send_inplane": send_inplane, "send_normal": send_normal, "embedding": embedding, "inverse_mass": inverse_mass, "radial_weight": radial_weight, "mix_weight": mix_weight, "self_weight": self_weight, "charge_weight": charge_weight, "readout_weight": readout_weight, "readout_vector": readout_vector, "kernel_filter": kernel_filter}


time_step = 0.5
width_x = 2.0
width_y = 4.0
width_z = 2.0
far_away = 1000.0
softening = 0.25
basis_reach = 6.0
envelope_reach = 4.0
highest = lax.Precision.HIGHEST

def wave_vectors(grid_side, layers, strips):
    wave_index = jnp.arange(grid_side ** 3)
    along_x = (wave_index // (grid_side * grid_side)).astype(jnp.float32) / (strips * width_x)
    along_y = (wave_index // grid_side % grid_side - grid_side // 2).astype(jnp.float32) / width_y
    along_z = (wave_index % grid_side - grid_side // 2).astype(jnp.float32) / (layers * width_z)
    wave_rows = 2.0 * jnp.pi * jnp.stack([along_x, along_y, along_z], axis=1)
    keeper = (wave_index != grid_side // 2 * grid_side + grid_side // 2).astype(jnp.float32)
    return (wave_rows, keeper)

def local_terms(ext_pos, ext_kind, ext_live, neighbour_rows, embedding, radial_weight, mix_weight, self_weight, readout_weight, readout_vector, charge_weight):
    own_atoms = neighbour_rows.shape[1]
    kind_values = jnp.arange(embedding.shape[0]).astype(jnp.float32)
    one_hot = (ext_kind[:, None] == kind_values[None, :]).astype(jnp.float32)
    embedded = jnp.dot(one_hot, embedding, precision=highest)
    outgoing = jnp.dot(embedded, mix_weight, precision=highest) * ext_live[:, None]
    centre = ext_pos[:, :own_atoms]
    partner = jnp.take(ext_pos, neighbour_rows, axis=1)
    offsets = partner - centre[:, None, :]
    distance = jnp.sqrt(lax.optimization_barrier(jnp.sum(offsets * offsets, axis=0)) + softening)
    basis_count = radial_weight.shape[0]
    spacing = basis_reach / (basis_count - 1)
    centres = spacing * jnp.arange(basis_count).astype(jnp.float32)
    scaled = (distance[None, :, :] - centres[:, None, None]) / spacing
    envelope = 1.0 / (1.0 + (distance / envelope_reach) ** 4)
    radial_basis = jnp.exp(-scaled * scaled) * envelope[None, :, :]
    filters = jnp.einsum('bma,bc->mac', radial_basis, radial_weight, precision=highest)
    gathered = jnp.take(outgoing, neighbour_rows, axis=0)
    message = lax.optimization_barrier(jnp.sum(filters * gathered, axis=0))
    hidden = jax.nn.silu(jnp.dot(embedded[:own_atoms], self_weight, precision=highest) + message)
    own_live = ext_live[:own_atoms]
    readout = jnp.dot(jax.nn.silu(jnp.dot(hidden, readout_weight, precision=highest)), readout_vector, precision=highest)
    charges = jnp.dot(hidden, charge_weight, precision=highest) * own_live[:, None]
    return (jnp.sum(readout * own_live), charges)

def structure_terms(wave_rows, own_pos, charges):
    phase = jnp.dot(wave_rows, own_pos, precision=highest)
    cosine_sum = jnp.dot(jnp.cos(phase), charges, precision=highest)
    sine_sum = jnp.dot(jnp.sin(phase), charges, precision=highest)
    return (cosine_sum, sine_sum)

def pick_slots(table, slot_rows):
    return jnp.take_along_axis(table, slot_rows[None], axis=3)

def build_records(moved, species, counts, send_inplane, send_normal):
    live_slots = (jnp.arange(ATOMS_DEV)[None, :] < counts[:, None]).astype(jnp.float32).reshape(-1)
    records = jnp.concatenate([moved, species.astype(jnp.float32)[None, :], live_slots[None, :]], axis=0)
    records = records.reshape(5, N_GZ, N_XY, ATOMS_DEV)
    inplane_lists = send_inplane.reshape(2, N_GZ, N_XY, GXY)
    to_lower = pick_slots(records, inplane_lists[0])
    to_upper = pick_slots(records, inplane_lists[1])
    strip_index = jnp.arange(N_XY)
    box_x = N_XY * width_x
    row_pick = (jnp.arange(5) == 0).astype(jnp.float32)[:, None, None, None]
    at_start = (strip_index == 0).astype(jnp.float32)[None, None, :, None]
    at_end = (strip_index == N_XY - 1).astype(jnp.float32)[None, None, :, None]
    from_lower = jnp.roll(to_upper, 1, axis=2) - row_pick * box_x * at_start
    from_upper = jnp.roll(to_lower, -1, axis=2) + row_pick * box_x * at_end
    first_section = jnp.concatenate([records, from_lower, from_upper], axis=3)
    normal_lists = send_normal.reshape(2, N_GZ, N_XY, GGZ)
    to_below = pick_slots(first_section, normal_lists[0])
    to_above = pick_slots(first_section, normal_lists[1])
    zero_layer = jnp.zeros_like(to_below[:, :1])
    from_below = jnp.concatenate([zero_layer, to_above[:, :-1]], axis=1)
    from_above = jnp.concatenate([to_below[:, 1:], zero_layer], axis=1)
    padding = jnp.array([far_away, far_away, far_away, 0.0, 0.0], dtype=jnp.float32)[:, None, None, None]
    padding = jnp.broadcast_to(padding, (5, N_GZ, N_XY, 1))
    return jnp.concatenate([first_section, from_below, from_above, padding], axis=3)

def total_energy(moved, species, counts, neighbours, send_inplane, send_normal, embedding, radial_weight, mix_weight, self_weight, charge_weight, readout_weight, readout_vector, kernel_filter):
    extended = build_records(moved, species, counts, send_inplane, send_normal)
    domain_count = N_GZ * N_XY
    per_domain = jnp.moveaxis(extended.reshape(5, domain_count, EXT), 1, 0)
    domain_lists = jnp.moveaxis(neighbours.reshape(NEIGH, domain_count, ATOMS_DEV), 1, 0)
    wave_rows, keeper = wave_vectors(KGRID, N_GZ, N_XY)

    def one_domain(running, pieces):
        record, neighbour_rows = pieces
        local_sum, charges = local_terms(record[:3], record[3], record[4], neighbour_rows, embedding, radial_weight, mix_weight, self_weight, readout_weight, readout_vector, charge_weight)
        cosine_part, sine_part = structure_terms(wave_rows, record[:3, :ATOMS_DEV], charges)
        return ((running[0] + local_sum, running[1] + cosine_part, running[2] + sine_part), None)
    start_values = (jnp.zeros((), jnp.float32), jnp.zeros((NK, C), jnp.float32), jnp.zeros((NK, C), jnp.float32))
    finals, unused = lax.scan(jax.checkpoint(one_domain), start_values, (per_domain, domain_lists))
    local_total, cosine_sum, sine_sum = finals
    ewald = jnp.sum(keeper[:, None] * kernel_filter * (cosine_sum * cosine_sum + sine_sum * sine_sum)) / (2.0 * ATOMS)
    return local_total + ewald

def reference(positions, velocities, forces, species, counts, neighbours, send_inplane, send_normal, embedding, inverse_mass, radial_weight, mix_weight, self_weight, charge_weight, readout_weight, readout_vector, kernel_filter):
    mass_factor = inverse_mass[species]
    half_velocity = velocities + 0.5 * time_step * forces * mass_factor[None, :]
    moved = positions + time_step * half_velocity

    def energy_of(moved_now):
        return total_energy(moved_now, species, counts, neighbours, send_inplane, send_normal, embedding, radial_weight, mix_weight, self_weight, charge_weight, readout_weight, readout_vector, kernel_filter)
    energy_total, pullback = jax.vjp(energy_of, moved)
    gradient = pullback(jnp.ones((), jnp.float32))[0]
    forces_new = -gradient
    velocities_new = half_velocity + 0.5 * time_step * forces_new * mass_factor[None, :]
    return (moved, velocities_new, forces_new, energy_total / ATOMS)
```

```python
import jax
import jax.numpy as jnp
from jax import lax
from jax.experimental import pallas as pl
from jax.experimental.pallas import tpu as pltpu
from jax.sharding import PartitionSpec as P

MESH = pl.DeviceIdType.MESH
F32 = jnp.float32
BF16 = jnp.bfloat16

KGRID = 8
NX = 4
NY = 8
NZ = 8
N_GZ = 16
N_XY = 32
ATOMS = 65536.0
OWN = 128
NEIGH = 24
NB = 16
SPECIES = 4
SLOTS = 384
HALF = 32
CHUNK = 4
ZERO_TILE = 4
ZERO_ROW = 4

time_step = 0.5
width_x = 2.0
width_y = 4.0
width_z = 2.0
far_away = 1000.0
softening = 0.25
spacing = 6.0 / (NB - 1)
envelope_reach = 4.0

NN = (((1,), (0,)), ((), ()))
NT = (((1,), (1,)), ((), ()))


def split(value):
    high = value.astype(BF16)
    return high, (value - high.astype(F32)).astype(BF16)


def mm(a, b, dims=NN):
    def one(left, right):
        return lax.dot_general(left, right, dims, preferred_element_type=F32)

    return one(a[0], b[0]) + (one(a[0], b[1]) + one(a[1], b[0]))


def iota(shape, dim):
    return lax.broadcasted_iota(jnp.int32, shape, dim)


def sigmoid(value):
    return 1.0 / (1.0 + jnp.exp(-value))


def rows_of(values):
    return jnp.broadcast_to(values, (8, values.shape[1]))


def take(table, index):
    return jnp.take_along_axis(table, index, axis=1, mode="promise_in_bounds")


def kernel(
    counts_ref,
    mass_ref,
    pos_ref,
    vel_ref,
    force_ref,
    kind_ref,
    neigh_ref,
    sendp_ref,
    sendn_ref,
    emb_ref,
    radial_ref,
    mix_ref,
    self_ref,
    charge_ref,
    readout_ref,
    vector_ref,
    filter_ref,
    pos_out,
    vel_out,
    force_out,
    energy_out,
    rec,
    rec_other,
    idx_p,
    idx_n,
    out_p,
    in_p,
    out_n,
    in_n,
    q_out,
    q_in,
    part,
    gather_1,
    swap_2,
    swap_3,
    final,
    grad_out,
    grad_in,
    misc_out,
    misc_in,
    back_n_out,
    back_n_in,
    back_p_out,
    back_p_in,
    slopes,
    units,
    codes,
    trig_q,
    trig_pt,
    hot,
    send_sem,
    recv_sem,
):
    gz = lax.axis_index("gz")
    xy = lax.axis_index("xy")
    core = lax.rem(gz, 2)
    z = lax.div(gz, 2)
    x = lax.rem(xy, NX)
    y = lax.div(xy, NX)

    partner = (gz + 1 - 2 * core, xy)
    z_peers = [(2 * lax.rem(z + d, NZ) + core, xy) for d in range(1, NZ)]
    y_peers = [(gz, NX * lax.rem(y + d, NY) + x) for d in range(1, NY)]
    x_peers = [(gz, NX * y + lax.rem(x + d, NX)) for d in range(1, NX)]
    p_lower = (gz, lax.rem(xy + N_XY - 1, N_XY))
    p_upper = (gz, lax.rem(xy + 1, N_XY))
    g_lower = (lax.rem(gz + N_GZ - 1, N_GZ), xy)
    g_upper = (lax.rem(gz + 1, N_GZ), xy)

    barrier = pltpu.get_barrier_semaphore()
    greeted = [partner, p_lower, p_upper, g_lower, g_upper] + z_peers + y_peers + x_peers
    for device in greeted:
        pl.semaphore_signal(barrier, inc=1, device_id=device, device_id_type=MESH)

    counter = [0]

    def send(src, dst, device):
        slot = counter[0]
        counter[0] += 1
        copy = pltpu.make_async_remote_copy(
            src_ref=src,
            dst_ref=dst,
            send_sem=send_sem.at[slot],
            recv_sem=recv_sem.at[slot],
            device_id=device,
            device_id_type=MESH,
        )
        copy.start()
        return copy

    started = []

    kind = kind_ref[...]
    mass_row = jnp.where(
        kind == 0,
        mass_ref[0],
        jnp.where(kind == 1, mass_ref[1], jnp.where(kind == 2, mass_ref[2], mass_ref[3])),
    )
    half_velocity = vel_ref[...] + (0.5 * time_step) * force_ref[...] * mass_row
    moved = pos_ref[...] + time_step * half_velocity
    pos_out[...] = moved
    lane = iota((8, OWN), 1)
    sub = iota((8, OWN), 0)
    live = (lane < counts_ref[0]).astype(F32)
    rec[...] = jnp.zeros((8, OWN), F32)
    rec[0:3, :] = moved
    rec[3:4, :] = kind.astype(F32)
    rec[4:5, :] = live[0:1, :]
    own = rec[...]

    idx_p[...] = jnp.zeros((1, OWN), jnp.int32)
    idx_p[0:1, 0:32] = sendp_ref[1:2, :]
    idx_p[0:1, 32:64] = sendp_ref[0:1, :]
    idx_n[0:1, 0:64] = sendn_ref[0:1, :]
    idx_n[0:1, 64:128] = sendn_ref[1:2, :]
    index_p = rows_of(idx_p[...])
    index_n = rows_of(idx_n[...])

    out_p[...] = take(own, index_p)

    pl.semaphore_wait(barrier, len(greeted))
    up = send(out_p, in_p.at[0], p_upper)
    down = send(out_p, in_p.at[1], p_lower)
    mate = send(rec, rec_other, partner)
    started += [up, down, mate]

    embedding = split(
        jnp.concatenate([emb_ref[...], jnp.zeros((4, 128), F32)], axis=0)
    )
    mixed = mm(embedding, split(mix_ref[...]))
    selfed = mm(embedding, split(self_ref[...]))
    radial = radial_ref[...]
    weights = jnp.concatenate([radial * mixed[s : s + 1, :] for s in range(SPECIES)], axis=0)
    weights_all = split(jnp.concatenate([weights, selfed], axis=0))
    weights = (weights_all[0][0 : SPECIES * NB], weights_all[1][0 : SPECIES * NB])

    up.wait_recv()
    down.wait_recv()
    shift = (sub == 0).astype(F32) * (N_XY * width_x)
    from_lower = in_p[0] - jnp.where(xy == 0, shift, jnp.zeros_like(shift))
    from_upper = in_p[1] + jnp.where(xy == N_XY - 1, shift, jnp.zeros_like(shift))
    tile_1 = jnp.where(lane < 32, from_lower, from_upper)
    low = jnp.bitwise_and(index_n, 127)
    out_n[...] = jnp.where(index_n < OWN, take(own, low), take(tile_1, low))
    below = send(out_n, in_n.at[1], g_lower)
    above = send(out_n, in_n.at[0], g_upper)
    started += [below, above]

    mate.wait_recv()
    both = jnp.concatenate([own, rec_other[...]], axis=1)
    steps = iota((8, 2 * OWN), 0).astype(F32)

    def circle(turns):
        angle = (2.0 * jnp.pi) * (turns - jnp.floor(turns + 0.5))
        return jnp.cos(angle), jnp.sin(angle)

    cos_x, sin_x = circle(both[0:1, :] * (steps / (N_XY * width_x)))
    cos_y, sin_y = circle(both[1:2, :] * ((steps - KGRID // 2) / width_y))
    cos_z, sin_z = circle(
        both[2:3, :] * ((steps - KGRID // 2) / (N_GZ * width_z)) - 0.25 * core.astype(F32)
    )
    cos_z = cos_z * both[4:5, :]
    sin_z = sin_z * both[4:5, :]
    pairs = []
    for k in range(KGRID):
        cy, sy = cos_y[k : k + 1, :], sin_y[k : k + 1, :]
        pairs.append((cy * cos_z - sy * sin_z, sy * cos_z + cy * sin_z))
    wave_p = []
    for k in range(KGRID):
        cx, sx = cos_x[k : k + 1, :], sin_x[k : k + 1, :]
        for j in range(KGRID):
            c, s = pairs[j]
            wave_p.append(cx * c - sx * s)
            trig_q[k * KGRID + j] = -(sx * c + cx * s)
    wave_p = jnp.concatenate(wave_p, axis=0)

    below.wait_recv()
    above.wait_recv()
    pad_column = jnp.where(sub < 3, far_away, 0.0)
    zeros = jnp.zeros((8, OWN), F32)
    from_below = jnp.where(gz == 0, zeros, in_n[0])
    from_above = jnp.where(gz == N_GZ - 1, zeros, in_n[1])
    tile_1 = jnp.where(lane < 64, tile_1, from_below)
    tile_2 = jnp.where(lane < 64, from_above, pad_column)

    bases = iota((NB, OWN), 0).astype(F32)
    sums = [jnp.zeros((NB, OWN), F32) for _ in range(SPECIES)]
    for m in range(NEIGH):
        index = rows_of(neigh_ref[m : m + 1, :])
        low = jnp.bitwise_and(index, 127)
        found = jnp.where(
            index < OWN,
            take(own, low),
            jnp.where(index < 2 * OWN, take(tile_1, low), take(tile_2, low)),
        )
        offset = found - own
        square = offset * offset
        distance = jnp.sqrt(square[0:1] + square[1:2] + square[2:3] + softening)
        units[m] = jnp.where(sub < 3, offset / distance, 0.0)
        code = jnp.where(found[4:5] > 0.5, found[3:4], -1.0)
        codes[m : m + 1, :] = code
        ratio = distance / envelope_reach
        cube = ratio * ratio * ratio
        envelope = 1.0 / (1.0 + ratio * cube)
        scaled = distance / spacing - bases
        basis = jnp.exp(-scaled * scaled) * envelope
        slopes[m] = basis * ((-2.0 / spacing) * scaled - envelope * cube)
        for s in range(SPECIES):
            sums[s] = sums[s] + jnp.where(code == float(s), basis, 0.0)

    kind_row = own[3:4, :]
    hot_kind = (kind_row == sub.astype(F32)).astype(F32)
    mixing = jnp.concatenate(sums + [hot_kind], axis=0)
    before = mm(split(mixing.T), weights_all)
    gate = sigmoid(before)
    hidden = before * gate
    hidden_slope = gate * (1.0 + before * (1.0 - gate))
    hidden_2 = split(hidden)
    charge_w = split(charge_ref[...])
    charges = mm(hidden_2, charge_w)
    q_out[...] = charges
    mate_q = send(q_out, q_in, partner)
    started += [mate_q]

    readout_w = split(readout_ref[...])
    ahead = mm(hidden_2, readout_w)
    gate = sigmoid(ahead)
    live_column = (iota((OWN, 128), 0) < counts_ref[0]).astype(F32)
    vector = vector_ref[...]
    atom_row = jnp.sum(ahead * gate * live_column, axis=0, keepdims=True) * vector
    ahead_grad = live_column * vector * (gate * (1.0 + ahead * (1.0 - gate)))

    mate_q.wait_recv()
    q_both = jnp.concatenate([charges, q_in[...]], axis=0)
    q_pair = split(q_both)
    partial = mm(split(wave_p), q_pair)
    part[...] = partial.reshape(KGRID * KGRID, 8, 128)
    part[ZERO_TILE] = jnp.where(sub == ZERO_ROW, atom_row, part[ZERO_TILE])

    colours = ((0, z, z_peers, NZ, y, y_peers), (1, y, y_peers, NY, z, z_peers))
    phase = []
    for colour, me, peers, size, _, _ in colours:
        base = colour * HALF
        copies = []
        for d in range(1, size):
            start = base + CHUNK * lax.rem(me + d, size)
            copies.append(
                send(part.at[pl.ds(start, CHUNK)], gather_1.at[colour, d - 1], peers[d - 1])
            )
        phase.append(copies)
        started += copies

    hidden_grad = mm(split(ahead_grad), readout_w, NT)
    trig_t = split(wave_p.T)
    trig_pt[0] = trig_t[0]
    trig_pt[1] = trig_t[1]
    q_t = split(q_both.T)
    rows = iota((SLOTS, OWN), 0)
    for m in range(NEIGH):
        hot[:, m * OWN : (m + 1) * OWN] = (
            (neigh_ref[m : m + 1, :] == rows).astype(F32).astype(BF16)
        )

    swap = []
    for colour, me, peers, size, other, other_peers in colours:
        for copy in phase[colour]:
            copy.wait_recv()
        total = part[pl.ds(colour * HALF + CHUNK * me, CHUNK)]
        for d in range(1, size):
            total = total + gather_1[colour, d - 1]
        swap_2[colour, other] = total
        copies = [
            send(swap_2.at[colour, other], swap_2.at[colour, other], device)
            for device in other_peers
        ]
        swap.append(copies)
        started += copies
    last = []
    for colour, me, peers, size, other, other_peers in colours:
        for copy in swap[colour]:
            copy.wait_recv()
        total = swap_2[colour, 0]
        for d in range(1, NY):
            total = total + swap_2[colour, d]
        swap_3[colour, x] = total
        copies = [
            send(swap_3.at[colour, x], swap_3.at[colour, x], device) for device in x_peers
        ]
        last.append(copies)
        started += copies
    spread = []
    for colour, me, peers, size, other, other_peers in colours:
        for copy in last[colour]:
            copy.wait_recv()
        total = swap_3[colour, 0]
        for d in range(1, NX):
            total = total + swap_3[colour, d]
        place = pl.ds(colour * HALF + CHUNK * me, CHUNK)
        final[place] = total
        copies = [send(final.at[place], final.at[place], device) for device in peers]
        spread += copies
        started += copies
    for copy in spread:
        copy.wait_recv()

    keep = 1.0 - ((iota((64, 8, 128), 0) == ZERO_TILE) & (iota((64, 8, 128), 1) == ZERO_ROW)).astype(F32)
    structure = final[...]
    wave_weight = keep * filter_ref[...] * structure / ATOMS
    ewald = 0.5 * jnp.sum(wave_weight * structure, axis=0)
    ewald = ewald + jnp.where(sub == ZERO_ROW, final[ZERO_TILE], 0.0)
    ewald = jnp.sum(ewald, axis=0, keepdims=True)
    weight_2 = split(wave_weight.reshape(512, 128))
    charge_grad = mm((trig_pt[0], trig_pt[1]), weight_2)
    along = mm(weight_2, q_t).reshape(KGRID, KGRID, 8, 2 * OWN)
    phase_grad = along * trig_q[...].reshape(KGRID, KGRID, 8, 2 * OWN)
    by_x = jnp.sum(phase_grad, axis=1)
    by_y = jnp.sum(phase_grad, axis=0)
    along_x = sum(float(k) * by_x[k] for k in range(1, KGRID))
    along_y = sum(float(k - KGRID // 2) * by_y[k] for k in range(KGRID) if k != KGRID // 2)
    along_z = jnp.sum(by_y, axis=0) * (steps - KGRID // 2)

    def down_rows(value, factor):
        return jnp.sum(value, axis=0, keepdims=True) * (2.0 * jnp.pi * factor)

    wave_grad = jnp.concatenate(
        [
            down_rows(along_x, 1.0 / (N_XY * width_x)),
            down_rows(along_y, 1.0 / width_y),
            down_rows(along_z, 1.0 / (N_GZ * width_z)),
            jnp.zeros((5, 2 * OWN), F32),
        ],
        axis=0,
    )
    grad_out[...] = charge_grad[OWN:, :]
    misc_out[0] = wave_grad[:, OWN:]
    misc_out[1] = rows_of(ewald)
    mate_g = send(grad_out, grad_in, partner)
    mate_m = send(misc_out, misc_in, partner)
    started += [mate_g, mate_m]
    mate_g.wait_recv()
    mate_m.wait_recv()
    charge_grad = charge_grad[0:OWN, :] + grad_in[...]
    wave_grad = wave_grad[:, 0:OWN] + misc_in[0]
    energy = jnp.sum(ewald + misc_in[1, 0:1, :], axis=1, keepdims=True)
    energy_out[...] = energy / ATOMS

    hidden_grad = hidden_grad + mm(split(charge_grad), charge_w, NT)
    before_grad = hidden_grad * hidden_slope
    mixing_grad = mm(weights, split(before_grad), NT)
    pulls = [mixing_grad[s * NB : (s + 1) * NB, :] for s in range(SPECIES)]
    own_grad = jnp.zeros((8, OWN), F32)
    spread_sum = jnp.zeros((16, SLOTS), F32)
    columns = []
    for m in range(NEIGH):
        code = codes[m : m + 1, :]
        pull = jnp.where(code == 0.0, pulls[0], 0.0)
        for s in range(1, SPECIES):
            pull = jnp.where(code == float(s), pulls[s], pull)
        along_pair = jnp.sum(pull * slopes[m], axis=0, keepdims=True)
        push = units[m] * along_pair
        own_grad = own_grad - push
        high, small = split(push)
        columns.append(jnp.concatenate([high, small], axis=0))
    columns = jnp.concatenate(columns, axis=1)
    spread_sum = lax.dot_general(columns, hot[...], NT, preferred_element_type=F32)
    spread_sum = spread_sum[0:8] + spread_sum[8:16]

    back_n_out[0] = spread_sum[:, OWN : 2 * OWN]
    back_n_out[1] = spread_sum[:, 2 * OWN :]
    to_below = send(back_n_out.at[0], back_n_in.at[0], g_lower)
    to_above = send(back_n_out.at[1], back_n_in.at[1], g_upper)
    started += [to_below, to_above]
    hot_n = (iota((2 * OWN, OWN), 0) == idx_n[...]).astype(F32).astype(BF16)
    hot_p = ((iota((OWN, OWN), 0) == idx_p[...]) & (iota((OWN, OWN), 1) < 64)).astype(F32).astype(BF16)
    to_below.wait_recv()
    to_above.wait_recv()
    came = jnp.where(
        lane < 64,
        jnp.where(gz == 0, zeros, back_n_in[1]),
        jnp.where(gz == N_GZ - 1, zeros, back_n_in[0]),
    )

    def scatter(value, table):
        high, small = split(value)
        both = lax.dot_general(
            jnp.concatenate([high, small], axis=0), table, NT, preferred_element_type=F32
        )
        return both[0:8] + both[8:16]

    section = spread_sum[:, 0 : 2 * OWN] + scatter(came, hot_n)
    back_p_out[...] = section[:, OWN:]
    to_lower = send(back_p_out, back_p_in.at[0], p_lower)
    to_upper = send(back_p_out, back_p_in.at[1], p_upper)
    started += [to_lower, to_upper]
    own_grad = own_grad + section[:, 0:OWN] + wave_grad
    to_lower.wait_recv()
    to_upper.wait_recv()
    came = jnp.where(lane < 32, back_p_in[0], jnp.where(lane < 64, back_p_in[1], zeros))
    own_grad = own_grad + scatter(came, hot_p)
    forces_new = -own_grad[0:3, :]
    force_out[...] = forces_new
    vel_out[...] = half_velocity + (0.5 * time_step) * forces_new * mass_row

    for copy in started:
        copy.wait_send()


COPIES = 11 + 2 * (2 * 7 + 7 + 3)


def local(
    positions,
    velocities,
    forces,
    species,
    counts,
    neighbours,
    send_inplane,
    send_normal,
    embedding,
    inverse_mass,
    radial_weight,
    mix_weight,
    self_weight,
    charge_weight,
    readout_weight,
    readout_vector,
    kernel_filter,
):
    vmem = pl.BlockSpec(memory_space=pltpu.VMEM)
    smem = pl.BlockSpec(memory_space=pltpu.SMEM)
    tile = (8, 128)
    out = pl.pallas_call(
        kernel,
        out_shape=(
            jax.ShapeDtypeStruct((3, OWN), F32),
            jax.ShapeDtypeStruct((3, OWN), F32),
            jax.ShapeDtypeStruct((3, OWN), F32),
            jax.ShapeDtypeStruct((1, 1), F32),
        ),
        in_specs=[smem, smem] + [vmem] * 15,
        out_specs=(vmem, vmem, vmem, vmem),
        scratch_shapes=[
            pltpu.VMEM(tile, F32),
            pltpu.VMEM(tile, F32),
            pltpu.VMEM((1, 128), jnp.int32),
            pltpu.VMEM((1, 128), jnp.int32),
            pltpu.VMEM(tile, F32),
            pltpu.VMEM((2, 8, 128), F32),
            pltpu.VMEM(tile, F32),
            pltpu.VMEM((2, 8, 128), F32),
            pltpu.VMEM((128, 128), F32),
            pltpu.VMEM((128, 128), F32),
            pltpu.VMEM((64, 8, 128), F32),
            pltpu.VMEM((2, 7, CHUNK, 8, 128), F32),
            pltpu.VMEM((2, 8, CHUNK, 8, 128), F32),
            pltpu.VMEM((2, 4, CHUNK, 8, 128), F32),
            pltpu.VMEM((64, 8, 128), F32),
            pltpu.VMEM((128, 128), F32),
            pltpu.VMEM((128, 128), F32),
            pltpu.VMEM((2, 8, 128), F32),
            pltpu.VMEM((2, 8, 128), F32),
            pltpu.VMEM((2, 8, 128), F32),
            pltpu.VMEM((2, 8, 128), F32),
            pltpu.VMEM(tile, F32),
            pltpu.VMEM((2, 8, 128), F32),
            pltpu.VMEM((NEIGH, NB, 128), F32),
            pltpu.VMEM((NEIGH, 8, 128), F32),
            pltpu.VMEM((NEIGH, 128), F32),
            pltpu.VMEM((64, 8, 256), F32),
            pltpu.VMEM((2, 256, 512), BF16),
            pltpu.VMEM((SLOTS, NEIGH * OWN), BF16),
            pltpu.SemaphoreType.DMA((COPIES + 8,)),
            pltpu.SemaphoreType.DMA((COPIES + 8,)),
        ],
        compiler_params=pltpu.CompilerParams(
            collective_id=0, has_side_effects=True
        ),
    )(
        counts,
        inverse_mass,
        positions,
        velocities,
        forces,
        species.reshape(1, OWN),
        neighbours,
        send_inplane,
        send_normal,
        embedding,
        radial_weight,
        mix_weight,
        self_weight,
        charge_weight,
        readout_weight,
        readout_vector.reshape(1, 128),
        kernel_filter.reshape(64, 8, 128),
    )
    return out[0], out[1], out[2], out[3].reshape(())


def solution(mesh):
    return jax.shard_map(
        local,
        mesh=mesh,
        in_specs=(
            P(None, ("gz", "xy")),
            P(None, ("gz", "xy")),
            P(None, ("gz", "xy")),
            P(("gz", "xy")),
            P(("gz", "xy")),
            P(None, ("gz", "xy")),
            P(None, ("gz", "xy")),
            P(None, ("gz", "xy")),
            P(),
            P(),
            P(),
            P(),
            P(),
            P(),
            P(),
            P(),
            P(),
        ),
        out_specs=(P(None, ("gz", "xy")), P(None, ("gz", "xy")), P(None, ("gz", "xy")), P()),
        check_vma=False,
    )
```
